128 devices in a mesh: grp: 4 (over x_hi, core), blk: 32 (over x_lo, z, y).
Axes of the slice: x: 4 (x_hi: 2, x_lo: 2; x = x_hi * 2 + x_lo), y: 4, z: 4, core: 2. Of those that a mesh axis runs over, the one named last changes fastest.
Arguments:
- fine_coef: float32 [512, 20, 32, 128], P(('grp', 'blk')), may hold values from -6 to 6
- src_fine: int32 [1024], P(('grp', 'blk')), may hold values from 0 to 3
- target_group: int32 [1024], P(('grp', 'blk')), may hold values from 0 to 4, as said below
- slot: int32 [1024], P(('grp', 'blk')), may hold values from 0 to 15
- valence_intersection: float32 [2048, 20, 20], P(('grp', 'blk')), may hold values from -0.5 to 0.5
- conduction_intersection: float32 [2048, 32, 32], P(('grp', 'blk')), may hold values from -1 to 1
- kernel: float32 [128, 4, 640, 640], P(('grp', 'blk')), may hold values from -0.125 to 0.125
- energies: float32 [128, 640], P(('grp', 'blk')), may hold values from 0.5 to 2
Outputs:
- applied: float32 [128, 640, 128], P(('grp', 'blk'))
The draws below stay inside these ranges and needn't reach their ends.
Inputs may be any that keep to these rules, and one draw needn't show every extreme that they name: `src_fine`: an index among the 4 fine momenta of the device that holds the entry. `slot`: an index among the 16 intersection slots of the device that holds the entry. `target_group`: the value 4 marks an unused entry; in each device's 8 entries the used ones come first, at least 2 of them, and some device uses all.
All inputs are finite; a program needn't handle non-finite values.
Results may differ from the reference program's by a relative error of at most 0.0003.
Values sent between devices are 32-bit elements; how exact they have to be, the bound alone decides.
A program may use at most 64 MiB of HBM per device.

```python
import math
import jax
import jax.numpy as jnp
from jax import lax

NV = 20
NC = 32
NVEC = 128
STOPS = 4
F_DEV = 4
E_DEV = 8
W_DEV = 16
PAIRS = 640
FINE = 512
ENTRIES = 1024
SLOTS = 2048
NQ = 128
N_GRP = 4
N_BLK = 32
DEVICES = 128


def draw_target_group(key, part):
    first_key, second_key = jax.random.split(jax.random.fold_in(key, 11))
    chosen = jax.random.randint(first_key, (DEVICES, E_DEV), 0, N_GRP)
    used = jax.random.randint(second_key, (DEVICES,), E_DEV // 4, E_DEV + 1)
    used = used.at[0].set(E_DEV)
    position = jnp.arange(E_DEV, dtype=jnp.int32)[None, :]
    marked = jnp.where(position < used[:, None], chosen, N_GRP)
    return marked.reshape(DEVICES * E_DEV).astype(jnp.int32)


def place_ends(result, rng, least, high):
    place = [jax.random.randint(jax.random.fold_in(rng, axis), (), 0, length) for axis, length in enumerate(result.shape)]
    longest = result.shape.index(max(result.shape))
    next_to = place[:longest] + [(place[longest] + 1) % result.shape[longest]] + place[longest + 1:]
    return result.at[tuple(place)].set(least).at[tuple(next_to)].set(high)


def levels(key, dims, cuts, low, high):
    level = 1.0
    for axis_at, parts in cuts:
        steps = jax.random.uniform(jax.random.fold_in(jax.random.fold_in(key, 6), axis_at), (parts,), jnp.float32, low / len(cuts), high / len(cuts))
        level = level * jnp.repeat(jnp.exp(steps), dims[axis_at] // parts).reshape((-1,) + (1,) * (len(dims) - 1 - axis_at))
    return level


def normal_values(stream_key, extent, spread, reach, shards=(), held_as=jnp.bfloat16):
    array = jax.random.normal(stream_key, extent, jnp.float32) * spread
    if len(shards) > 0:
        array = levels(stream_key, extent, shards, -0.22, 0.18) * array
    return jnp.clip(array, min=-reach, max=reach).astype(held_as)


def setup_inputs(seed: int = 0) -> dict:
    keys = jax.random.split(jax.random.key(seed), 9)
    fine_coef = normal_values(keys[0], (FINE, NV, NC, NVEC), 1.0, 6.0, ((0, 128),), jnp.float32)
    src_fine = place_ends(jax.random.randint(keys[1], (ENTRIES,), 0, F_DEV), jax.random.fold_in(keys[1], 1), 0, F_DEV - 1).astype(jnp.int32)
    target_group = draw_target_group(jax.random.fold_in(keys[8], 71), 0)
    slot = place_ends(jax.random.randint(keys[3], (ENTRIES,), 0, W_DEV), jax.random.fold_in(keys[3], 1), 0, W_DEV - 1).astype(jnp.int32)
    valence_intersection = normal_values(keys[4], (SLOTS, NV, NV), (NV * E_DEV) ** -0.5, 0.5, ((0, 128),), jnp.float32)
    conduction_intersection = normal_values(keys[5], (SLOTS, NC, NC), NC ** -0.5, 1.0, ((0, 128),), jnp.float32)
    kernel = normal_values(keys[6], (NQ, STOPS, PAIRS, PAIRS), (STOPS * PAIRS) ** -0.5, 0.125, ((0, 128),), jnp.float32)
    energies = jnp.clip(jnp.exp(math.log(2.0) - 1.3862944 * jax.random.uniform(keys[7], (NQ, PAIRS), jnp.float32) ** levels(keys[7], (NQ, PAIRS), ((0, 128),), -0.2, 0.2)), 0.5, 2.0)
    return dict(fine_coef=fine_coef, src_fine=src_fine, target_group=target_group, slot=slot, valence_intersection=valence_intersection, conduction_intersection=conduction_intersection, kernel=kernel, energies=energies)


def rotate_entries(fine_part, src_part, target_part, slot_part, valence_part, conduction_part):
    entries = src_part.shape[0]
    block_size = 8
    src_rows = src_part.reshape(entries // block_size, block_size)
    target_rows = target_part.reshape(entries // block_size, block_size)
    slot_rows = slot_part.reshape(entries // block_size, block_size)
    totals = jnp.zeros((N_GRP, NV, NC, NVEC), jnp.float32)

    def advance(totals, pieces):
        src_now, target_now, slot_now = pieces
        gathered = jnp.take(fine_part, src_now, axis=0).astype(jnp.float32)
        val_now = jnp.take(valence_part, slot_now, axis=0).astype(jnp.float32)
        cond_now = jnp.take(conduction_part, slot_now, axis=0).astype(jnp.float32)
        partial_value = jnp.einsum("evw,evcn->ewcn", val_now, gathered, precision=lax.Precision.HIGHEST)
        rotated = jnp.einsum("ecd,ewcn->ewdn", cond_now, partial_value, precision=lax.Precision.HIGHEST)
        selector = (target_now[:, None] == jnp.arange(N_GRP, dtype=jnp.int32)[None, :]).astype(jnp.float32)
        totals = totals + jnp.einsum("eg,ewdn->gwdn", selector, rotated, precision=lax.Precision.HIGHEST)
        return totals, None

    totals, unused = lax.scan(advance, totals, (src_rows, target_rows, slot_rows))
    return totals


def reference(fine_coef, src_fine, target_group, slot, valence_intersection, conduction_intersection, kernel, energies):
    coarse = jnp.zeros((N_BLK, N_GRP, NV, NC, NVEC), jnp.float32)

    def add_device(device, coarse):
        device = jnp.asarray(device).astype(jnp.int32)
        fine_part = lax.dynamic_slice_in_dim(fine_coef, (device * F_DEV).astype(jnp.int32), F_DEV, 0)
        src_part = lax.dynamic_slice_in_dim(src_fine, (device * E_DEV).astype(jnp.int32), E_DEV, 0)
        target_part = lax.dynamic_slice_in_dim(target_group, (device * E_DEV).astype(jnp.int32), E_DEV, 0)
        slot_part = lax.dynamic_slice_in_dim(slot, (device * E_DEV).astype(jnp.int32), E_DEV, 0)
        valence_part = lax.dynamic_slice_in_dim(valence_intersection, (device * W_DEV).astype(jnp.int32), W_DEV, 0)
        conduction_part = lax.dynamic_slice_in_dim(conduction_intersection, (device * W_DEV).astype(jnp.int32), W_DEV, 0)
        totals = rotate_entries(fine_part, src_part, target_part, slot_part, valence_part, conduction_part)
        column = (device % N_BLK).astype(jnp.int32)
        return coarse.at[column].add(totals)

    coarse = lax.fori_loop(0, N_GRP * N_BLK, add_device, coarse)
    coarse = jnp.transpose(coarse, (1, 0, 2, 3, 4)).reshape(N_GRP, N_BLK, NV * NC, NVEC)
    flat = coarse.reshape(N_GRP * N_BLK, NV * NC, NVEC)
    applied = energies.astype(jnp.float32)[:, :, None] * flat
    for offset in range(STOPS):
        moved = jnp.roll(coarse, offset, axis=1).reshape(N_GRP * N_BLK, NV * NC, NVEC)
        applied = applied + jnp.einsum("qpr,qrn->qpn", kernel[:, offset].astype(jnp.float32), moved, precision=lax.Precision.HIGHEST)
    return applied
```

```python
import jax
import jax.numpy as jnp
from jax import lax
from jax.experimental import pallas as pl
from jax.experimental.pallas import tpu as pltpu
from jax.sharding import PartitionSpec as P

MESH = pl.DeviceIdType.MESH
F32 = jnp.float32
BF16 = jnp.bfloat16

NV, NC, NVEC = 20, 32, 128
PAIRS = NV * NC
ENT, FINE, SLOTS, GROUPS, STOPS = 8, 4, 16, 4, 4
CHUNKS = 5
ROWS = PAIRS // CHUNKS
VE = NV * ENT

CORE_REM, CORE_OWN, ACROSS, UP, RING = 0, 1, 2, 3, 3
FLOWS = 7
LAG = 2


def split(value):
    high = value.astype(BF16)
    low = (value - high.astype(F32)).astype(BF16)
    return high, low


def kernel(
    src_hbm, tgt_hbm, slot_hbm, val_hbm, cond_hbm, en_hbm, x_hbm, k_hbm, out_ref,
    src_s, tgt_s, slot_s, val, cond, en, x, xh, xl, z, ovs, t, r_rem, r_own, p_buf, r_x, c_buf, g_buf,
    kf, kh, kl, acc, lsem, send, recv,
):
    grp = lax.axis_index("grp")
    blk = lax.axis_index("blk")
    core = lax.rem(grp, 2)
    xhi = grp // 2
    y = lax.rem(blk, 4)
    row0 = blk - y
    level = lax.rem(blk // 4, 4)
    mate = (xhi * 2 + 1 - core, blk)
    far = ((1 - xhi) * 2 + core, blk)
    above = (grp, lax.rem(blk + 4, 32))
    below = (grp, lax.rem(blk + 28, 32))
    ring = [None] + [(grp, row0 + lax.rem(y + s, 4)) for s in (1, 2, 3)]

    local = [
        pltpu.make_async_copy(src_hbm, src_s, lsem.at[11]),
        pltpu.make_async_copy(tgt_hbm, tgt_s, lsem.at[12]),
        pltpu.make_async_copy(slot_hbm, slot_s, lsem.at[13]),
        pltpu.make_async_copy(cond_hbm, cond, lsem.at[0]),
        pltpu.make_async_copy(val_hbm, val, lsem.at[1]),
        pltpu.make_async_copy(en_hbm, en, lsem.at[2]),
    ]
    xin = [pltpu.make_async_copy(x_hbm.at[f], x.at[f], lsem.at[3 + f]) for f in range(FINE)]
    kin = [pltpu.make_async_copy(k_hbm.at[0, s], kf.at[s], lsem.at[7 + s]) for s in range(STOPS)]
    for copy in local + xin:
        copy.start()

    barrier = pltpu.get_barrier_semaphore()
    for dev in (mate, far, below, ring[1], ring[2], ring[3]):
        pl.semaphore_signal(barrier, inc=1, device_id=dev, device_id_type=MESH)
    for copy in kin:
        copy.start()

    for i in (0, 1, 2, 4):
        local[i].wait()
    for e in range(ENT):
        ovs[pl.ds(e, NV, stride=ENT), :] = val[pl.ds(slot_s[e], NV, stride=SLOTS), :]
    pick = (
        lax.rem(lax.broadcasted_iota(jnp.int32, (GROUPS * NV, NV), 0), NV)
        == lax.broadcasted_iota(jnp.int32, (GROUPS * NV, NV), 1)
    ).astype(F32)
    ov_rows = ovs[...]
    ov3 = jnp.concatenate([ov_rows, ov_rows, ov_rows], axis=0)
    nt = (((1,), (1,)), ((), ()))
    wide = lax.dot_general(pick, ov3, nt, precision=lax.Precision.HIGHEST, preferred_element_type=F32)
    lane = lax.broadcasted_iota(jnp.int32, (GROUPS * NV, 3 * VE), 1)
    group = lax.broadcasted_iota(jnp.int32, (GROUPS * NV, 3 * VE), 0) // NV
    entry = lax.rem(lane, ENT)
    target = jnp.full((GROUPS * NV, 3 * VE), GROUPS, jnp.int32)
    for e in range(ENT):
        target = jnp.where(entry == e, tgt_s[e], target)
    wide = jnp.where(target == group, wide, 0.0)
    wide_h = wide.astype(BF16)
    wide_l = wide - wide_h.astype(F32)
    w_lhs = jnp.where(lane < 2 * VE, wide_h.astype(F32), wide_l).astype(BF16)

    for f in range(FINE):
        xin[f].wait()
        h, l = split(x[f])
        xh[f] = h
        xl[f] = l

    local[3].wait()
    eye = (
        lax.broadcasted_iota(jnp.int32, (NC, NC), 0) == lax.broadcasted_iota(jnp.int32, (NC, NC), 1)
    ).astype(F32)
    clane = lax.broadcasted_iota(jnp.int32, (NC, 3 * NC), 1)
    for e in range(ENT):
        oc = cond[slot_s[e]]
        oct3 = lax.dot_general(
            eye, jnp.concatenate([oc, oc, oc], axis=0), nt,
            precision=lax.Precision.HIGHEST, preferred_element_type=F32,
        )
        oct_h = oct3.astype(BF16).astype(F32)
        o_lhs = jnp.where(clane < 2 * NC, oct_h, oct3 - oct_h).astype(BF16)
        hh = xh[src_s[e]]
        ll = xl[src_s[e]]
        for v in range(0, NV, 2):
            cols = []
            for u in (v, v + 1):
                a = hh[u * NC:(u + 1) * NC]
                cols.append(jnp.concatenate([a, ll[u * NC:(u + 1) * NC], a], axis=0))
            both = jnp.concatenate(cols, axis=1)
            res = jnp.dot(o_lhs, both, preferred_element_type=F32)
            z[pl.ds((v * ENT + e) * NC, NC), :] = res[:, :NVEC]
            z[pl.ds(((v + 1) * ENT + e) * NC, NC), :] = res[:, NVEC:]

    for c in range(0, NC, 2):
        cols = []
        for u in (c, c + 1):
            h, l = split(z[pl.ds(u, VE, stride=NC), :])
            cols.append(jnp.concatenate([h, l, h], axis=0))
        res = jnp.dot(w_lhs, jnp.concatenate(cols, axis=1), preferred_element_type=F32)
        t[pl.ds(c, GROUPS * NV, stride=NC), :] = res[:, :NVEC]
        t[pl.ds(c + 1, GROUPS * NV, stride=NC), :] = res[:, NVEC:]

    pl.semaphore_wait(barrier, 6)

    def chunk(k):
        return pl.ds(k * ROWS, ROWS)

    def t_rows(h, k):
        return pl.ds(pl.multiple_of(h * PAIRS + k * ROWS, ROWS), ROWS)

    def remote(src, dst, flow, k, dev):
        return pltpu.make_async_remote_copy(
            src_ref=src, dst_ref=dst, send_sem=send.at[flow, k], recv_sem=recv.at[flow, k],
            device_id=dev, device_id_type=MESH,
        )

    h_own = grp
    h_far = (1 - xhi) * 2 + core
    h_mate = xhi * 2 + 1 - core
    h_far_mate = (1 - xhi) * 2 + 1 - core

    def core_rem(k):
        return remote(t.at[t_rows(h_far_mate, k)], r_rem.at[chunk(k)], CORE_REM, k, mate)

    def core_own(k):
        return remote(t.at[t_rows(h_mate, k)], r_own.at[chunk(k)], CORE_OWN, k, mate)

    def across(k):
        return remote(p_buf.at[chunk(k)], r_x.at[chunk(k)], ACROSS, k, far)

    def up(k):
        return remote(c_buf.at[0, chunk(k)], c_buf.at[1, chunk(k)], UP, k, above)

    def around(s, k):
        held = (y + s) // 4
        return remote(c_buf.at[held, chunk(k)], g_buf.at[s - 1, chunk(k)], RING + s, k, ring[s])

    for k in range(CHUNKS):
        core_rem(k).start()
    for k in range(CHUNKS):
        core_own(k).start()
    for k in range(CHUNKS):
        core_rem(k).wait_recv()
        p_buf[chunk(k)] = t[t_rows(h_far, k)] + r_rem[chunk(k)]
        across(k).start()

    local[5].wait()
    for copy in kin:
        copy.wait()
    diagonal = (
        lax.broadcasted_iota(jnp.int32, (ROWS, ROWS), 0) == lax.broadcasted_iota(jnp.int32, (ROWS, ROWS), 1)
    )

    def split_kernel(k):
        cols = pl.ds(k * ROWS, ROWS)
        kf[0, cols, cols] = kf[0, cols, cols] + jnp.where(diagonal, en[:, cols], 0.0)

        def body(s, carry):
            h, l = split(kf[s, :, cols])
            kh[s, k] = h
            kl[s, k] = l
            return carry

        lax.fori_loop(0, STOPS, body, 0)

    def multiply(s, k, value):
        h, l = split(value)
        first = jnp.dot(kh[s, k], jnp.concatenate([h, l], axis=1), preferred_element_type=F32)
        second = jnp.dot(kl[s, k], h, preferred_element_type=F32)
        total = first[:, :NVEC] + first[:, NVEC:] + second
        if s == 0 and k == 0:
            acc[...] = total
        else:
            acc[...] = acc[...] + total

    def forward(k):
        @pl.when(y >= 1)
        def _():
            up(k).wait_recv()
            for s in (1, 2, 3):
                @pl.when(y + s >= 4)
                def _():
                    around(s, k).start()

    for k in range(CHUNKS):
        core_own(k).wait_recv()
        across(k).wait_recv()
        owned = t[t_rows(h_own, k)] + r_own[chunk(k)] + r_x[chunk(k)]
        c_buf[0, chunk(k)] = owned

        @pl.when(y >= 1)
        def _():
            up(k).start()

        for s in (1, 2, 3):
            @pl.when(y + s < 4)
            def _():
                around(s, k).start()

        if k >= LAG:
            @pl.when(level != 0)
            def _():
                forward(k - LAG)

        split_kernel(k)
    for k in range(CHUNKS):
        if k < CHUNKS - LAG:
            @pl.when(level == 0)
            def _():
                forward(k)
        else:
            forward(k)
    for k in range(CHUNKS):
        multiply(0, k, c_buf[0, chunk(k)])
    for k in range(CHUNKS):
        for s in (1, 3, 2):
            around(s, k).wait_recv()
            multiply(s, k, g_buf[s - 1, chunk(k)])
    out_ref[0] = acc[...]

    for k in range(CHUNKS):
        core_rem(k).wait_send()
        core_own(k).wait_send()
        across(k).wait_send()

        @pl.when(y >= 1)
        def _():
            up(k).wait_send()

        for s in (1, 2, 3):
            around(s, k).wait_send()


def on_device(fine_coef, src_fine, target_group, slot, valence, conduction, kernel_blocks, energies):
    hbm = pl.BlockSpec(memory_space=pltpu.HBM)
    dma = pltpu.SemaphoreType.DMA
    block = (PAIRS, NVEC)
    return pl.pallas_call(
        kernel,
        name="apply",
        out_shape=jax.ShapeDtypeStruct((1, PAIRS, NVEC), F32),
        in_specs=[hbm] * 8,
        out_specs=pl.BlockSpec(memory_space=pltpu.VMEM),
        scratch_shapes=[
            pltpu.SMEM((ENT,), jnp.int32),
            pltpu.SMEM((ENT,), jnp.int32),
            pltpu.SMEM((ENT,), jnp.int32),
            pltpu.VMEM((NV * SLOTS, NV), F32),
            pltpu.VMEM((SLOTS, NC, NC), F32),
            pltpu.VMEM((1, PAIRS), F32),
            pltpu.VMEM((FINE, PAIRS, NVEC), F32),
            pltpu.VMEM((FINE, PAIRS, NVEC), BF16),
            pltpu.VMEM((FINE, PAIRS, NVEC), BF16),
            pltpu.VMEM((VE * NC, NVEC), F32),
            pltpu.VMEM((VE, NV), F32),
            pltpu.VMEM((GROUPS * PAIRS, NVEC), F32),
            pltpu.VMEM(block, F32),
            pltpu.VMEM(block, F32),
            pltpu.VMEM(block, F32),
            pltpu.VMEM(block, F32),
            pltpu.VMEM((2,) + block, F32),
            pltpu.VMEM((3,) + block, F32),
            pltpu.VMEM((STOPS, PAIRS, PAIRS), F32),
            pltpu.VMEM((STOPS, CHUNKS, PAIRS, ROWS), BF16),
            pltpu.VMEM((STOPS, CHUNKS, PAIRS, ROWS), BF16),
            pltpu.VMEM(block, F32),
            dma((14,)),
            dma((FLOWS, CHUNKS)),
            dma((FLOWS, CHUNKS)),
        ],
        compiler_params=pltpu.CompilerParams(
            collective_id=0, has_side_effects=True, vmem_limit_bytes=56 << 20
        ),
    )(
        src_fine, target_group, slot,
        valence.transpose(1, 0, 2).reshape(NV * SLOTS, NV), conduction, energies,
        fine_coef.reshape(FINE, PAIRS, NVEC), kernel_blocks,
    )


def solution(mesh):
    spec = ("grp", "blk")
    return jax.shard_map(
        on_device,
        mesh=mesh,
        in_specs=(
            P(spec, None, None, None), P(spec), P(spec), P(spec), P(spec, None, None),
            P(spec, None, None), P(spec, None, None, None), P(spec, None),
        ),
        out_specs=P(spec, None, None),
        check_vma=False,
    )
```

```python
import jax
import jax.numpy as jnp
from jax import lax
from jax.experimental import pallas as pl
from jax.experimental.pallas import tpu as pltpu
from jax.sharding import PartitionSpec as P

def swap(a):
    return jnp.swapaxes(a, 0, 1)


MESH = pl.DeviceIdType.MESH
F32 = jnp.float32
BF16 = jnp.bfloat16

NV, NC, NVEC = 20, 32, 128
PAIRS = NV * NC
ENT, FINE, SLOTS, GROUPS, STOPS = 8, 4, 16, 4, 4
CHUNKS = 5
ROWS = PAIRS // CHUNKS
WIDE = NV // CHUNKS
VE = NV * ENT

CORE_REM, CORE_OWN, ACROSS, UP, RING = 0, 1, 2, 3, 3
FLOWS = 7
LAG = 1
FLIGHT = 3


def split(value):
    high = value.astype(BF16)
    low = (value - high.astype(F32)).astype(BF16)
    return high, low


def kernel(
    src_hbm, tgt_hbm, slot_hbm, val_hbm, cond_hbm, en_hbm, x_hbm, k_hbm, out_ref,
    src_s, tgt_s, slot_s, val, cond, en, x, xh, xl, z, ovs, t, r_rem, r_own, p_buf, r_x, c_buf, g_buf,
    kf, kh, kl, acc, lsem, send, recv,
):
    grp = lax.axis_index("grp")
    blk = lax.axis_index("blk")
    core = lax.rem(grp, 2)
    xhi = grp // 2
    y = lax.rem(blk, 4)
    row0 = blk - y
    level = lax.rem(blk // 4, 4)
    mate = (xhi * 2 + 1 - core, blk)
    far = ((1 - xhi) * 2 + core, blk)
    above = (grp, lax.rem(blk + 4, 32))
    below = (grp, lax.rem(blk + 28, 32))
    ring = [None] + [(grp, row0 + lax.rem(y + s, 4)) for s in (1, 2, 3)]

    local = [
        pltpu.make_async_copy(src_hbm, src_s, lsem.at[11]),
        pltpu.make_async_copy(tgt_hbm, tgt_s, lsem.at[12]),
        pltpu.make_async_copy(slot_hbm, slot_s, lsem.at[13]),
        pltpu.make_async_copy(cond_hbm, cond, lsem.at[0]),
        pltpu.make_async_copy(val_hbm, val, lsem.at[1]),
        pltpu.make_async_copy(en_hbm, en, lsem.at[2]),
    ]
    xin = [pltpu.make_async_copy(x_hbm.at[f], x.at[f], lsem.at[3 + f]) for f in range(FINE)]
    kin = [pltpu.make_async_copy(k_hbm.at[0, s], kf.at[s], lsem.at[7 + s]) for s in range(STOPS)]
    for copy in local + xin:
        copy.start()

    barrier = pltpu.get_barrier_semaphore()
    for dev in (mate, far, below, ring[1], ring[2], ring[3]):
        pl.semaphore_signal(barrier, inc=1, device_id=dev, device_id_type=MESH)
    for i in (0, 1, 2, 4):
        local[i].wait()
    for e in range(ENT):
        ovs[pl.ds(e, NV, stride=ENT), :] = val[pl.ds(slot_s[e], NV, stride=SLOTS), :]
    pick = (
        lax.rem(lax.broadcasted_iota(jnp.int32, (GROUPS * NV, NV), 0), NV)
        == lax.broadcasted_iota(jnp.int32, (GROUPS * NV, NV), 1)
    ).astype(F32)
    ov_rows = ovs[...]
    ov3 = jnp.concatenate([ov_rows, ov_rows, ov_rows], axis=0)
    nt = (((1,), (1,)), ((), ()))
    wide = lax.dot_general(pick, ov3, nt, precision=lax.Precision.HIGHEST, preferred_element_type=F32)
    lane = lax.broadcasted_iota(jnp.int32, (GROUPS * NV, 3 * VE), 1)
    group = lax.broadcasted_iota(jnp.int32, (GROUPS * NV, 3 * VE), 0) // NV
    entry = lax.rem(lane, ENT)
    target = jnp.full((GROUPS * NV, 3 * VE), GROUPS, jnp.int32)
    for e in range(ENT):
        target = jnp.where(entry == e, tgt_s[e], target)
    wide = jnp.where(target == group, wide, 0.0)
    wide_h = wide.astype(BF16)
    wide_l = wide - wide_h.astype(F32)
    w_lhs = jnp.where(lane < 2 * VE, wide_h.astype(F32), wide_l).astype(BF16)

    local[3].wait()
    eye = (
        lax.broadcasted_iota(jnp.int32, (NC, NC), 0) == lax.broadcasted_iota(jnp.int32, (NC, NC), 1)
    ).astype(F32)
    clane = lax.broadcasted_iota(jnp.int32, (NC, 3 * NC), 1)
    o_lhs = []
    for e in range(ENT):
        oc = cond[slot_s[e]]
        oct3 = lax.dot_general(
            eye, jnp.concatenate([oc, oc, oc], axis=0), nt,
            precision=lax.Precision.HIGHEST, preferred_element_type=F32,
        )
        oct_h = oct3.astype(BF16).astype(F32)
        o_lhs.append(jnp.where(clane < 2 * NC, oct_h, oct3 - oct_h).astype(BF16))

    for f in range(FINE):
        xin[f].wait()
        h, l = split(x[f])
        xh[f] = h
        xl[f] = l
    for copy in kin:
        copy.start()

    for v in range(0, NV, 2):
        halves = ([], [])
        for e in range(ENT):
            cols = []
            for u in (v, v + 1):
                rows = pl.ds(u * NC, NC)
                a = xh[src_s[e], rows]
                cols.append(jnp.concatenate([a, xl[src_s[e], rows], a], axis=0))
            res = jnp.dot(o_lhs[e], jnp.concatenate(cols, axis=1), preferred_element_type=F32)
            halves[0].append(res[:, :NVEC])
            halves[1].append(res[:, NVEC:])
        for i in (0, 1):
            z[:, pl.ds((v + i) * ENT, ENT), :] = swap(jnp.stack(halves[i], axis=0))

    for c0 in range(0, NC, 8):
        parts = []
        for c in range(c0, c0 + 8, 2):
            cols = []
            for u in (c, c + 1):
                h, l = split(z[u])
                cols.append(jnp.concatenate([h, l, h], axis=0))
            res = jnp.dot(w_lhs, jnp.concatenate(cols, axis=1), preferred_element_type=F32)
            parts += [res[:, :NVEC], res[:, NVEC:]]
        t[:, pl.ds(c0, 8), :] = swap(jnp.stack(parts, axis=0))

    pl.semaphore_wait(barrier, 6)

    def chunk(k):
        return pl.ds(k * WIDE, WIDE)

    def t_rows(h, k):
        return pl.ds(h * NV + k * WIDE, WIDE)

    def remote(src, dst, flow, k, dev):
        return pltpu.make_async_remote_copy(
            src_ref=src, dst_ref=dst, send_sem=send.at[flow, k], recv_sem=recv.at[flow, k],
            device_id=dev, device_id_type=MESH,
        )

    h_own = grp
    h_far = (1 - xhi) * 2 + core
    h_mate = xhi * 2 + 1 - core
    h_far_mate = (1 - xhi) * 2 + 1 - core

    def core_rem(k):
        return remote(t.at[t_rows(h_far_mate, k)], r_rem.at[chunk(k)], CORE_REM, k, mate)

    def core_own(k):
        return remote(t.at[t_rows(h_mate, k)], r_own.at[chunk(k)], CORE_OWN, k, mate)

    def across(k):
        return remote(p_buf.at[chunk(k)], r_x.at[chunk(k)], ACROSS, k, far)

    def up(k):
        return remote(c_buf.at[0, chunk(k)], c_buf.at[1, chunk(k)], UP, k, above)

    def around(s, k):
        held = (y + s) // 4
        return remote(c_buf.at[held, chunk(k)], g_buf.at[s - 1, chunk(k)], RING + s, k, ring[s])

    for k in range(CHUNKS):
        core_rem(k).start()
    for k in range(CHUNKS):
        core_own(k).start()
    def send_across(k):
        core_rem(k).wait_recv()
        p_buf[chunk(k)] = t[t_rows(h_far, k)] + r_rem[chunk(k)]
        across(k).start()

    for k in range(FLIGHT):
        send_across(k)

    local[5].wait()
    for copy in kin:
        copy.wait()
    diagonal = (
        lax.broadcasted_iota(jnp.int32, (ROWS, ROWS), 0) == lax.broadcasted_iota(jnp.int32, (ROWS, ROWS), 1)
    )

    def split_kernel(k):
        cols = pl.ds(k * ROWS, ROWS)
        kf[0, cols, cols] = kf[0, cols, cols] + jnp.where(diagonal, en[:, cols], 0.0)

        def body(s, carry):
            h, l = split(kf[s, :, cols])
            kh[s, k] = h
            kl[s, k] = l
            return carry

        lax.fori_loop(0, STOPS, body, 0)

    def multiply(s, k, value):
        h, l = split(value)
        first = jnp.dot(kh[s, k], jnp.concatenate([h, l], axis=1), preferred_element_type=F32)
        second = jnp.dot(kl[s, k], h, preferred_element_type=F32)
        total = first[:, :NVEC] + first[:, NVEC:] + second
        if s == 0 and k == 0:
            acc[...] = total
        else:
            acc[...] = acc[...] + total

    def forward(k):
        @pl.when(y >= 1)
        def _():
            up(k).wait_recv()
            for s in (1, 2, 3):
                @pl.when(y + s >= 4)
                def _():
                    around(s, k).start()

    for k in range(CHUNKS):
        split_kernel(k)
    for k in range(CHUNKS):
        core_own(k).wait_recv()
        across(k).wait_recv()
        c_buf[0, chunk(k)] = t[t_rows(h_own, k)] + r_own[chunk(k)] + r_x[chunk(k)]

        @pl.when(y >= 1)
        def _():
            up(k).start()

        if k + FLIGHT < CHUNKS:
            send_across(k + FLIGHT)
        for s in (1, 2, 3):
            @pl.when(y + s < 4)
            def _():
                around(s, k).start()

        if k >= LAG:
            forward(k - LAG)
    for k in range(CHUNKS - LAG, CHUNKS):
        forward(k)
    for k in range(CHUNKS):
        multiply(0, k, c_buf[0, chunk(k)].reshape(ROWS, NVEC))
    for k in range(CHUNKS):
        for s in (1, 3, 2):
            around(s, k).wait_recv()
            multiply(s, k, g_buf[s - 1, chunk(k)].reshape(ROWS, NVEC))
    out_ref[0] = acc[...]

    for k in range(CHUNKS):
        core_rem(k).wait_send()
        core_own(k).wait_send()
        across(k).wait_send()

        @pl.when(y >= 1)
        def _():
            up(k).wait_send()

        for s in (1, 2, 3):
            around(s, k).wait_send()


def on_device(fine_coef, src_fine, target_group, slot, valence, conduction, kernel_blocks, energies):
    hbm = pl.BlockSpec(memory_space=pltpu.HBM)
    dma = pltpu.SemaphoreType.DMA
    block = (NV, NC, NVEC)
    return pl.pallas_call(
        kernel,
        name="apply",
        out_shape=jax.ShapeDtypeStruct((1, PAIRS, NVEC), F32),
        in_specs=[hbm] * 8,
        out_specs=pl.BlockSpec(memory_space=pltpu.VMEM),
        scratch_shapes=[
            pltpu.SMEM((ENT,), jnp.int32),
            pltpu.SMEM((ENT,), jnp.int32),
            pltpu.SMEM((ENT,), jnp.int32),
            pltpu.VMEM((NV * SLOTS, NV), F32),
            pltpu.VMEM((SLOTS, NC, NC), F32),
            pltpu.VMEM((1, PAIRS), F32),
            pltpu.VMEM((FINE, PAIRS, NVEC), F32),
            pltpu.VMEM((FINE, PAIRS, NVEC), BF16),
            pltpu.VMEM((FINE, PAIRS, NVEC), BF16),
            pltpu.VMEM((NC, VE, NVEC), F32),
            pltpu.VMEM((VE, NV), F32),
            pltpu.VMEM((GROUPS * NV, NC, NVEC), F32),
            pltpu.VMEM(block, F32),
            pltpu.VMEM(block, F32),
            pltpu.VMEM(block, F32),
            pltpu.VMEM(block, F32),
            pltpu.VMEM((2,) + block, F32),
            pltpu.VMEM((3,) + block, F32),
            pltpu.VMEM((STOPS, PAIRS, PAIRS), F32),
            pltpu.VMEM((STOPS, CHUNKS, PAIRS, ROWS), BF16),
            pltpu.VMEM((STOPS, CHUNKS, PAIRS, ROWS), BF16),
            pltpu.VMEM((PAIRS, NVEC), F32),
            dma((14,)),
            dma((FLOWS, CHUNKS)),
            dma((FLOWS, CHUNKS)),
        ],
        compiler_params=pltpu.CompilerParams(
            collective_id=0, has_side_effects=True, vmem_limit_bytes=56 << 20
        ),
    )(
        src_fine, target_group, slot,
        valence.transpose(1, 0, 2).reshape(NV * SLOTS, NV), conduction, energies,
        fine_coef.reshape(FINE, PAIRS, NVEC), kernel_blocks,
    )


def solution(mesh):
    spec = ("grp", "blk")
    return jax.shard_map(
        on_device,
        mesh=mesh,
        in_specs=(
            P(spec, None, None, None), P(spec), P(spec), P(spec), P(spec, None, None),
            P(spec, None, None), P(spec, None, None, None), P(spec, None),
        ),
        out_specs=P(spec, None, None),
        check_vma=False,
    )
```
